32 devices in a mesh: seq: 16 (over z, y, x), chan: 2 (over core).
Axes of the slice: x: 2, y: 2, z: 4, core: 2. Of those that a mesh axis runs over, the one named last changes fastest.
Arguments:
- inputs: float32 [256, 8192], P('chan', 'seq'), may hold values from -6 to 6
- value_weight: float32 [256, 256], P(None, 'chan'), may hold values from -0.375 to 0.375
- query_weight: float32 [256, 256], P(None, 'chan'), may hold values from -0.375 to 0.375
- filters: float32 [256, 8192], P('chan', 'seq'), may hold values from -1 to 1
- grad_out: float32 [256, 8192], P('chan', 'seq'), may hold values from -6 to 6
Outputs:
- input_grad: float32 [256, 8192], P('chan', 'seq')
- filter_grad: float32 [256, 8192], P('chan', 'seq')
- value_gradient: float32 [256, 256], P(None, 'chan')
- query_gradient: float32 [256, 256], P(None, 'chan')
The draws below stay inside these ranges and needn't reach their ends.
All inputs are finite; a program needn't handle non-finite values.
Results may differ from the reference program's by a relative error of at most 0.00018.
Values sent between devices are 32-bit elements; how exact they have to be, the bound alone decides.
A program may use at most 64 MiB of HBM per device.

```python
import math
import jax
import jax.numpy as jnp
from jax import lax

C = 256
SEQ = 8192


def draw_filters(key, part):
    rate_key = jax.random.fold_in(key, 11)
    noise_key = jax.random.fold_in(key, 12)
    log_rate = jax.random.uniform(rate_key, (C, 1), jnp.float32, math.log(0.5 / SEQ), math.log(1.0 / 40.0))
    noise = jnp.clip(jax.random.normal(noise_key, (C, SEQ), jnp.float32), -4.0, 4.0)
    decay_rate = jnp.exp(log_rate)
    lag_values = jnp.arange(SEQ, dtype=jnp.float32)[None, :]
    energy = jnp.expm1(-2.0 * decay_rate * SEQ) / jnp.expm1(-2.0 * decay_rate)
    return noise * jnp.exp(-decay_rate * lag_values) / jnp.sqrt(energy)


def steps_of(own_key, extent, cuts, least, high):
    factor_of, own = 1.0, jax.random.fold_in(own_key, 6)
    for axis_at, parts in cuts:
        steps = jnp.exp(jax.random.uniform(jax.random.fold_in(own, axis_at), (parts,), jnp.float32, least / len(cuts), high / len(cuts)))
        factor_of = factor_of * jnp.repeat(steps, extent[axis_at] // parts).reshape([-1 if axis == axis_at else 1 for axis in range(len(extent))])
    return factor_of


def centred(stream_key, shape, width, reach, pieces=(), kind=jnp.bfloat16):
    level = steps_of(stream_key, shape, pieces, -0.22, 0.18) if pieces else 1.0
    array = jax.random.normal(stream_key, shape, jnp.float32) * width * level
    return jnp.minimum(jnp.maximum(array, -reach), reach).astype(kind)


def setup_inputs(seed: int = 0) -> dict:
    key_of = jax.random.split(jax.random.key(seed), 6)
    inputs = centred(key_of[0], (C, SEQ), 1.0, 6.0, ((0, 2), (1, 16)), jnp.float32)
    value_weight = centred(key_of[1], (C, C), C ** -0.5, 0.375, ((1, 2),), jnp.float32)
    query_weight = centred(key_of[2], (C, C), C ** -0.5, 0.375, ((1, 2),), jnp.float32)
    filters = draw_filters(jax.random.fold_in(key_of[5], 71), 0)
    grad_out = centred(key_of[4], (C, SEQ), 1.0, 6.0, ((0, 2), (1, 16)), jnp.float32)
    return dict(inputs=inputs, value_weight=value_weight, query_weight=query_weight, filters=filters, grad_out=grad_out)


def correlate(blocks):
    projected, filters, gated_grad = blocks
    seq_length = projected.shape[1]
    padded = 2 * seq_length
    value_spec = jnp.fft.rfft(projected, n=padded, axis=1)
    filter_spec = jnp.fft.rfft(filters, n=padded, axis=1)
    grad_spec = jnp.fft.rfft(gated_grad, n=padded, axis=1)
    convolved = jnp.fft.irfft(filter_spec * value_spec, n=padded, axis=1)[:, :seq_length]
    grad_value = jnp.fft.irfft(jnp.conj(filter_spec) * grad_spec, n=padded, axis=1)[:, :seq_length]
    filter_grad = jnp.fft.irfft(jnp.conj(value_spec) * grad_spec, n=padded, axis=1)[:, :seq_length]
    return jnp.stack([convolved, grad_value, filter_grad])


def reference(inputs, value_weight, query_weight, filters, grad_out):
    precise = lax.Precision.HIGHEST
    channel_count = inputs.shape[0]
    seq_length = inputs.shape[1]
    grad_scale = seq_length ** -0.5
    projected = jnp.dot(value_weight.T, inputs, precision=precise, preferred_element_type=jnp.float32)
    query_proj = jnp.dot(query_weight.T, inputs, precision=precise, preferred_element_type=jnp.float32)
    gated_grad = grad_out * query_proj
    group_count = channel_count // 16
    results = lax.map(correlate, (projected.reshape(group_count, 16, seq_length), filters.reshape(group_count, 16, seq_length), gated_grad.reshape(group_count, 16, seq_length)))
    convolved = results[:, 0].reshape(channel_count, seq_length)
    grad_value = results[:, 1].reshape(channel_count, seq_length)
    filter_grad = results[:, 2].reshape(channel_count, seq_length) * grad_scale
    grad_query = grad_out * convolved
    input_grad = jnp.dot(value_weight, grad_value, precision=precise, preferred_element_type=jnp.float32) + jnp.dot(query_weight, grad_query, precision=precise, preferred_element_type=jnp.float32)
    value_gradient = jnp.dot(inputs, grad_value.T, precision=precise, preferred_element_type=jnp.float32) * grad_scale
    query_gradient = jnp.dot(inputs, grad_query.T, precision=precise, preferred_element_type=jnp.float32) * grad_scale
    return (input_grad, filter_grad, value_gradient, query_gradient)
```

```python
import functools
import math

import jax
import jax.numpy as jnp
import numpy as np
from jax import lax
from jax.experimental import pallas as pl
from jax.experimental.pallas import tpu as pltpu
from jax.sharding import PartitionSpec as P

BLK = 64
LANES = 128
GROUP = 8


HIGHEST = lax.Precision.HIGHEST


def complex_table(row_count, col_count, period, direction):
    row_iota = lax.broadcasted_iota(jnp.int32, (row_count, col_count), 0)
    col_iota = lax.broadcasted_iota(jnp.int32, (row_count, col_count), 1)
    rotation = 2.0 * math.pi / period * (row_iota * col_iota % period).astype(jnp.float32)
    cosine = jnp.cos(rotation)
    sine_part = direction * jnp.sin(rotation)
    upper_rows = jnp.stack([cosine, sine_part], axis=1)
    lower_rows = jnp.stack([-sine_part, cosine], axis=1)
    return jnp.stack([upper_rows, lower_rows], axis=0)


def rotate(columns, cosine, sine_part):
    return jnp.stack(
        [columns[0] * cosine - columns[1] * sine_part, columns[0] * sine_part + columns[1] * cosine]
    )


def multiply(first_spec, second_spec, conjugate):
    imag_first = -first_spec[1] if conjugate else first_spec[1]
    return jnp.stack(
        [
            first_spec[0] * second_spec[0] - imag_first * second_spec[1],
            first_spec[0] * second_spec[1] + imag_first * second_spec[0],
        ]
    )


def block_angles(block_size, inner_size, seq_rows, direction):
    outer_iota = lax.broadcasted_iota(jnp.int32, (block_size, inner_size), 0)
    inner_iota = lax.broadcasted_iota(jnp.int32, (block_size, inner_size), 1)
    rotation = (
        direction
        * 2.0
        * math.pi
        / seq_rows
        * (outer_iota * inner_iota % seq_rows).astype(jnp.float32)
    )
    return (jnp.cos(rotation)[:, :, None], jnp.sin(rotation)[:, :, None])


def local_forward(columns, block_size):
    seq_rows = columns.shape[1]
    item_width = columns.shape[2]
    inner_size = seq_rows // block_size
    shaped = columns.reshape(2, block_size, inner_size, item_width)
    first_pass = jnp.einsum(
        "xabz,xayk->ykbz",
        shaped,
        complex_table(block_size, block_size, block_size, -1.0),
        precision=HIGHEST,
    )
    cosine, sine_part = block_angles(block_size, inner_size, seq_rows, -1.0)
    rotated = rotate(first_pass, cosine, sine_part)
    second = jnp.einsum(
        "ykbz,ybwm->wkmz",
        rotated,
        complex_table(inner_size, inner_size, inner_size, -1.0),
        precision=HIGHEST,
    )
    return second.reshape(2, seq_rows, item_width)


def local_inverse(columns, block_size):
    seq_rows = columns.shape[1]
    item_width = columns.shape[2]
    inner_size = seq_rows // block_size
    shaped = columns.reshape(2, block_size, inner_size, item_width)
    first_pass = jnp.einsum(
        "xkmz,xmyb->ykbz",
        shaped,
        complex_table(inner_size, inner_size, inner_size, 1.0),
        precision=HIGHEST,
    )
    cosine, sine_part = block_angles(block_size, inner_size, seq_rows, 1.0)
    rotated = rotate(first_pass, cosine, sine_part)
    second = jnp.einsum(
        "xkbz,xkya->yabz",
        rotated,
        complex_table(block_size, block_size, block_size, 1.0),
        precision=HIGHEST,
    )
    return second.reshape(2, seq_rows, item_width) * (1.0 / seq_rows)


def cross_transform(columns, dft_table):
    seq_rows = columns.shape[1]
    item_width = columns.shape[2]
    shaped = columns.reshape(2, 1, seq_rows, item_width)
    transformed = jnp.einsum(
        "xpjz,xpyk->ykjz",
        lax.all_to_all(shaped, "seq", split_axis=2, concat_axis=1, tiled=True),
        dft_table,
        precision=HIGHEST,
    )
    result = lax.all_to_all(transformed, "seq", split_axis=1, concat_axis=2, tiled=True)
    return result.reshape(2, seq_rows, item_width)


def shard_twiddle(columns, frequency, seq_length, direction):
    seq_rows = columns.shape[1]
    local_pos = jnp.arange(seq_rows, dtype=jnp.int32)
    rotation = (
        direction
        * 2.0
        * math.pi
        / seq_length
        * (local_pos * frequency % seq_length).astype(jnp.float32)
    )
    return rotate(columns, jnp.cos(rotation)[:, None], jnp.sin(rotation)[:, None])


def forward(columns, shard_index, devices, block_size):
    seq_length = columns.shape[1] * devices
    columns = cross_transform(columns, complex_table(devices, devices, devices, -1.0))
    columns = shard_twiddle(columns, shard_index, seq_length, -1.0)
    return local_forward(columns, block_size)


def inverse(columns, shard_index, devices, block_size):
    seq_length = columns.shape[1] * devices
    columns = local_inverse(columns, block_size)
    columns = shard_twiddle(columns, shard_index, seq_length, 1.0)
    columns = cross_transform(
        columns, complex_table(devices, devices, devices, 1.0) * (1.0 / devices)
    )
    return columns


def per_device(inputs, value_weight, query_weight, filters, grad_out):
    channel_count = filters.shape[0]
    seq_rows = filters.shape[1]
    devices = lax.axis_size("seq")
    shard_index = lax.axis_index("seq")
    seq_length = seq_rows * devices
    grad_scale = 1.0 / math.sqrt(seq_length)
    all_inputs = lax.all_gather(inputs, "chan", axis=0, tiled=True)
    projected = jnp.einsum("cd,ct->dt", value_weight, all_inputs, precision=HIGHEST)
    query_proj = jnp.einsum("cd,ct->dt", query_weight, all_inputs, precision=HIGHEST)
    gated_grad = grad_out * query_proj
    signals = jnp.stack([projected, filters, gated_grad])
    position = shard_index * seq_rows + jnp.arange(seq_rows, dtype=jnp.int32)
    twist_angle = 0.5 * math.pi / seq_length * position.astype(jnp.float32)
    cosine = jnp.cos(twist_angle)
    sine_part = jnp.sin(twist_angle)
    twisted = jnp.stack([signals * cosine, -signals * sine_part])
    columns = jnp.transpose(twisted, (0, 3, 1, 2)).reshape(2, seq_rows, 3 * channel_count)
    spectra = forward(columns, shard_index, devices, BLK).reshape(2, seq_rows, 3, channel_count)
    value_spec = spectra[:, :, 0]
    filter_spec = spectra[:, :, 1]
    grad_spec = spectra[:, :, 2]
    products = jnp.stack(
        [
            multiply(filter_spec, value_spec, False),
            multiply(filter_spec, grad_spec, True),
            multiply(value_spec, grad_spec, True),
        ],
        axis=2,
    )
    restored = inverse(
        products.reshape(2, seq_rows, 3 * channel_count), shard_index, devices, BLK
    ).reshape(2, seq_rows, 3, channel_count)
    combined = restored[0] * cosine[:, None, None] - restored[1] * sine_part[:, None, None]
    combined = jnp.transpose(combined, (1, 2, 0))
    convolved = combined[0]
    grad_value = combined[1]
    filter_grad = combined[2] * grad_scale
    grad_query = grad_out * convolved
    input_grad = lax.psum_scatter(
        jnp.dot(value_weight, grad_value, precision=HIGHEST, preferred_element_type=jnp.float32)
        + jnp.dot(query_weight, grad_query, precision=HIGHEST, preferred_element_type=jnp.float32),
        "chan",
        scatter_dimension=0,
        tiled=True,
    )
    partial_value = jnp.einsum("ct,dt->cd", all_inputs, grad_value, precision=HIGHEST) * grad_scale
    partial_query = jnp.einsum("ct,dt->cd", all_inputs, grad_query, precision=HIGHEST) * grad_scale
    value_gradient, query_gradient = lax.psum((partial_value, partial_query), "seq")
    return (input_grad, filter_grad, value_gradient, query_gradient)


NN = (((1,), (0,)), ((), ()))
NT = (((1,), (1,)), ((), ()))


def split_table(table):
    high = table.astype(jnp.bfloat16)
    low = (table - high.astype(np.float32)).astype(jnp.bfloat16)
    return high, low


@functools.lru_cache(maxsize=None)
def transform_tables(seq_length):
    outer = seq_length // LANES
    k = np.arange(outer, dtype=np.float64)
    a = np.arange(outer, dtype=np.float64)
    b = np.arange(LANES, dtype=np.float64)
    phase = 2 * np.pi * np.outer(4 * k + 1, a) % (2 * np.pi * 4 * outer) / (4 * outer)
    small = np.concatenate([np.cos(phase), -np.sin(phase)], axis=0)
    wide = np.kron(small, np.eye(GROUP)).astype(np.float32)
    angle = 2 * np.pi * np.repeat(np.outer(4 * k + 1, b), GROUP, axis=0) / (4 * seq_length)
    turn = np.stack([np.cos(angle), np.sin(angle)]).astype(np.float32)
    inner = 2 * np.pi * (np.outer(b, b) % LANES) / LANES
    c, s = np.cos(inner), np.sin(inner)
    ahead = np.block([[c, -s], [s, c]]).astype(np.float32)
    back = np.block([[c, s], [-s, c]]).astype(np.float32)
    return (
        *split_table(wide),
        *split_table(np.ascontiguousarray(wide.T) / np.float32(seq_length)),
        *split_table(ahead),
        *split_table(back),
        turn,
    )


def split(x):
    high = x.astype(jnp.bfloat16)
    return high, (x - high.astype(jnp.float32)).astype(jnp.bfloat16)


def dot3(first, second, dims=NN):
    def dot(x, y):
        return lax.dot_general(x, y, dims, preferred_element_type=jnp.float32)

    return dot(first[0], second[0]) + (dot(first[0], second[1]) + dot(first[1], second[0]))


def fused_kernel(
    devices,
    scale,
    x_ref,
    vw_ref,
    qw_ref,
    f_ref,
    g_ref,
    wide_h,
    wide_l,
    tall_h,
    tall_l,
    ahead_h,
    ahead_l,
    back_h,
    back_l,
    turn_ref,
    ig_out,
    fg_out,
    vg_out,
    qg_out,
    other_x,
    out_block,
    send_sig,
    in_sig,
    spec,
    out_sig,
    ret_sig,
    part,
    scat,
    red,
    gath,
    ig_send,
    ig_recv,
    ssem,
    rsem,
    csend,
    crecv,
):
    me = lax.axis_index("seq")
    chan = lax.axis_index("chan")
    half, width = x_ref.shape
    pieces = width // LANES
    rows = 2 * half // devices

    barrier = pltpu.get_barrier_semaphore()

    def greet(i, carry):
        pl.semaphore_signal(
            barrier,
            inc=1,
            device_id={"seq": lax.rem(me + i, devices)},
            device_id_type=pl.DeviceIdType.MESH,
        )
        return carry

    lax.fori_loop(1, devices, greet, 0)
    pl.semaphore_signal(
        barrier, inc=1, device_id={"chan": 1 - chan}, device_id_type=pl.DeviceIdType.MESH
    )

    own_rows = pl.ds(pl.multiple_of(chan * half, half), half)
    other_rows = pl.ds(pl.multiple_of((1 - chan) * half, half), half)
    own_x = split(x_ref[...])
    partial_value = dot3(split(vw_ref[own_rows, :].T), own_x)
    partial_query = dot3(split(qw_ref[own_rows, :].T), own_x)

    pl.semaphore_wait(barrier, devices)

    def exchange(index, src, dst):
        return pltpu.make_async_remote_copy(
            src_ref=src,
            dst_ref=dst,
            send_sem=csend.at[index],
            recv_sem=crecv.at[index],
            device_id={"chan": 1 - chan},
            device_id_type=pl.DeviceIdType.MESH,
        )

    def each(slot, src_of, dst_of, what):
        def step(i, carry):
            peer = lax.rem(me + i, devices)
            copy = pltpu.make_async_remote_copy(
                src_ref=src_of(peer),
                dst_ref=dst_of(),
                send_sem=ssem.at[slot, i],
                recv_sem=rsem.at[slot, i],
                device_id={"seq": peer},
                device_id_type=pl.DeviceIdType.MESH,
            )
            getattr(copy, what)()
            return carry

        lax.fori_loop(1, devices, step, 0)

    def group_rows(peer, count):
        return pl.ds(pl.multiple_of(peer * count, count), count)

    def out_way(slot, what):
        src = f_ref if slot == 0 else send_sig.at[slot - 1]
        each(slot, lambda p: src.at[group_rows(p, GROUP), :], lambda: in_sig.at[slot, me], what)

    def back_way(slot, what):
        each(
            3 + slot,
            lambda p: out_sig.at[slot, p],
            lambda: ret_sig.at[slot, group_rows(me, GROUP), :],
            what,
        )

    def scatter(slot, what):
        each(
            6 + slot,
            lambda p: part.at[slot, group_rows(p, rows), :],
            lambda: scat.at[slot, me],
            what,
        )

    def gather(slot, what):
        each(
            8 + slot,
            lambda p: red.at[slot],
            lambda: gath.at[slot, group_rows(me, rows), :],
            what,
        )

    give_x = exchange(0, x_ref, other_x)
    give_x.start()
    out_way(0, "start")
    in_sig[0, me] = f_ref[group_rows(me, GROUP), :]
    give_x.wait()

    far_x = split(other_x[...])
    send_sig[0] = partial_value + dot3(split(vw_ref[other_rows, :].T), far_x)
    out_way(1, "start")
    in_sig[1, me] = send_sig[0, group_rows(me, GROUP), :]
    query_proj = partial_query + dot3(split(qw_ref[other_rows, :].T), far_x)
    send_sig[1] = g_ref[...] * query_proj
    out_way(2, "start")
    in_sig[2, me] = send_sig[1, group_rows(me, GROUP), :]

    wide = (wide_h[...], wide_l[...])
    tall = (tall_h[...], tall_l[...])
    ahead = (ahead_h[...], ahead_l[...])
    back = (back_h[...], back_l[...])
    cosine = turn_ref[0]
    sine = turn_ref[1]
    count = cosine.shape[0]

    def transform(slot):
        signal = jnp.concatenate(
            [
                in_sig[slot, source, :, piece * LANES : (piece + 1) * LANES]
                for source in range(devices)
                for piece in range(pieces)
            ],
            axis=0,
        )
        first = dot3(wide, split(signal))
        real, imag = first[:count], first[count:]
        turned = jnp.concatenate(
            [real * cosine + imag * sine, imag * cosine - real * sine], axis=1
        )
        spec[slot] = dot3(split(turned), ahead)

    def restore(first, second, conjugate, slot):
        real_a, imag_a = spec[first, :, :LANES], spec[first, :, LANES:]
        real_b, imag_b = spec[second, :, :LANES], spec[second, :, LANES:]
        if conjugate:
            imag_a = -imag_a
        product = jnp.concatenate(
            [real_a * real_b - imag_a * imag_b, real_a * imag_b + imag_a * real_b], axis=1
        )
        inner = dot3(split(product), back)
        real, imag = inner[:, :LANES], inner[:, LANES:]
        turned = jnp.concatenate(
            [real * cosine - imag * sine, imag * cosine + real * sine], axis=0
        )
        signal = dot3(tall, split(turned))
        for target in range(devices):
            for piece in range(pieces):
                at = (target * pieces + piece) * GROUP
                out_sig[slot, target, :, piece * LANES : (piece + 1) * LANES] = signal[
                    at : at + GROUP
                ]
        back_way(slot, "start")
        ret_sig[slot, group_rows(me, GROUP), :] = out_sig[slot, me]

    out_way(0, "wait_recv")
    transform(0)
    out_way(1, "wait_recv")
    transform(1)
    restore(0, 1, False, 0)
    out_way(2, "wait_recv")
    transform(2)
    restore(0, 2, True, 1)
    restore(1, 2, True, 2)

    def weight_part(slot, grad):
        near = dot3(own_x2, grad, NT)
        far = dot3(far_x2, grad, NT)
        part[slot, own_rows, :] = near
        part[slot, other_rows, :] = far
        scatter(slot, "start")
        scat[slot, me] = part[slot, group_rows(me, rows), :]

    own_x2 = split(x_ref[...])
    far_x2 = split(other_x[...])
    back_way(0, "wait_recv")
    grad_query = split(g_ref[...] * ret_sig[0])
    weight_part(0, grad_query)
    near_grad = dot3(split(qw_ref[own_rows, :]), grad_query)
    far_grad = dot3(split(qw_ref[other_rows, :]), grad_query)
    back_way(1, "wait_recv")
    grad_value = split(ret_sig[1])
    ig_send[...] = far_grad + dot3(split(vw_ref[other_rows, :]), grad_value)
    give_ig = exchange(1, ig_send, ig_recv)
    give_ig.start()
    weight_part(1, grad_value)

    def reduce(slot):
        scatter(slot, "wait_recv")
        total = scat[slot, 0]
        for source in range(1, devices):
            total = total + scat[slot, source]
        red[slot] = total * scale
        gather(slot, "start")
        gath[slot, group_rows(me, rows), :] = red[slot]

    reduce(0)
    near_grad = near_grad + dot3(split(vw_ref[own_rows, :]), grad_value)
    reduce(1)
    give_ig.wait()
    ig_out[...] = near_grad + ig_recv[...]
    back_way(2, "wait_recv")
    fg_out[...] = ret_sig[2] * scale
    for slot, out in ((0, qg_out), (1, vg_out)):
        gather(slot, "wait_recv")
        out[...] = gath[slot]
    for slot in range(3):
        out_way(slot, "wait_send")
        back_way(slot, "wait_send")
    for slot in range(2):
        scatter(slot, "wait_send")
        gather(slot, "wait_send")


def fused_device(inputs, value_weight, query_weight, filters, grad_out):
    half, width = inputs.shape
    devices = lax.axis_size("seq")
    seq_length = width * devices
    depth = value_weight.shape[0]
    rows = depth // devices
    tables = transform_tables(seq_length)
    count = seq_length // LANES * GROUP
    vmem = pl.BlockSpec(memory_space=pltpu.VMEM)
    f32 = jnp.float32
    ig, fg, vg, qg = pl.pallas_call(
        functools.partial(fused_kernel, devices, 1.0 / math.sqrt(seq_length)),
        out_shape=(
            jax.ShapeDtypeStruct((half, width), f32),
            jax.ShapeDtypeStruct((half, width), f32),
            jax.ShapeDtypeStruct((depth, half), f32),
            jax.ShapeDtypeStruct((depth, half), f32),
        ),
        in_specs=[vmem] * (5 + len(tables)),
        out_specs=(vmem,) * 4,
        scratch_shapes=[
            pltpu.VMEM((half, width), f32),
            pltpu.VMEM((GROUP, LANES), f32),
            pltpu.VMEM((2, half, width), f32),
            pltpu.VMEM((3, devices, GROUP, width), f32),
            pltpu.VMEM((3, count, 2 * LANES), f32),
            pltpu.VMEM((3, devices, GROUP, width), f32),
            pltpu.VMEM((3, half, width), f32),
            pltpu.VMEM((2, depth, half), f32),
            pltpu.VMEM((2, devices, rows, half), f32),
            pltpu.VMEM((2, rows, half), f32),
            pltpu.VMEM((2, depth, half), f32),
            pltpu.VMEM((half, width), f32),
            pltpu.VMEM((half, width), f32),
            pltpu.SemaphoreType.DMA((10, devices)),
            pltpu.SemaphoreType.DMA((10, devices)),
            pltpu.SemaphoreType.DMA((2,)),
            pltpu.SemaphoreType.DMA((2,)),
        ],
        compiler_params=pltpu.CompilerParams(
            collective_id=0, has_side_effects=True, vmem_limit_bytes=56 * 1024 * 1024
        ),
    )(inputs, value_weight, query_weight, filters, grad_out, *(jnp.asarray(t) for t in tables))
    return ig, fg, vg, qg


def on_device(inputs, value_weight, query_weight, filters, grad_out):
    channel_count, width = filters.shape
    devices = lax.axis_size("seq")
    fits = (
        channel_count == GROUP * devices
        and channel_count == inputs.shape[0]
        and lax.axis_size("chan") == 2
        and width % LANES == 0
        and channel_count % LANES == 0
        and value_weight.shape[0] % (GROUP * devices) == 0
    )
    body = fused_device if fits else per_device
    return body(inputs, value_weight, query_weight, filters, grad_out)


def solution(mesh):
    return jax.shard_map(
        on_device,
        mesh=mesh,
        in_specs=(
            P("chan", "seq"),
            P(None, "chan"),
            P(None, "chan"),
            P("chan", "seq"),
            P("chan", "seq"),
        ),
        out_specs=(P("chan", "seq"), P("chan", "seq"), P(None, "chan"), P(None, "chan")),
        check_vma=False,
    )
```

```python
import functools
import math

import jax
import jax.numpy as jnp
import numpy as np
from jax import lax
from jax.experimental import pallas as pl
from jax.experimental.pallas import tpu as pltpu
from jax.sharding import PartitionSpec as P

BLK = 64
LANES = 128
GROUP = 8


HIGHEST = lax.Precision.HIGHEST


def complex_table(row_count, col_count, period, direction):
    row_iota = lax.broadcasted_iota(jnp.int32, (row_count, col_count), 0)
    col_iota = lax.broadcasted_iota(jnp.int32, (row_count, col_count), 1)
    rotation = 2.0 * math.pi / period * (row_iota * col_iota % period).astype(jnp.float32)
    cosine = jnp.cos(rotation)
    sine_part = direction * jnp.sin(rotation)
    upper_rows = jnp.stack([cosine, sine_part], axis=1)
    lower_rows = jnp.stack([-sine_part, cosine], axis=1)
    return jnp.stack([upper_rows, lower_rows], axis=0)


def rotate(columns, cosine, sine_part):
    return jnp.stack(
        [columns[0] * cosine - columns[1] * sine_part, columns[0] * sine_part + columns[1] * cosine]
    )


def multiply(first_spec, second_spec, conjugate):
    imag_first = -first_spec[1] if conjugate else first_spec[1]
    return jnp.stack(
        [
            first_spec[0] * second_spec[0] - imag_first * second_spec[1],
            first_spec[0] * second_spec[1] + imag_first * second_spec[0],
        ]
    )


def block_angles(block_size, inner_size, seq_rows, direction):
    outer_iota = lax.broadcasted_iota(jnp.int32, (block_size, inner_size), 0)
    inner_iota = lax.broadcasted_iota(jnp.int32, (block_size, inner_size), 1)
    rotation = (
        direction
        * 2.0
        * math.pi
        / seq_rows
        * (outer_iota * inner_iota % seq_rows).astype(jnp.float32)
    )
    return (jnp.cos(rotation)[:, :, None], jnp.sin(rotation)[:, :, None])


def local_forward(columns, block_size):
    seq_rows = columns.shape[1]
    item_width = columns.shape[2]
    inner_size = seq_rows // block_size
    shaped = columns.reshape(2, block_size, inner_size, item_width)
    first_pass = jnp.einsum(
        "xabz,xayk->ykbz",
        shaped,
        complex_table(block_size, block_size, block_size, -1.0),
        precision=HIGHEST,
    )
    cosine, sine_part = block_angles(block_size, inner_size, seq_rows, -1.0)
    rotated = rotate(first_pass, cosine, sine_part)
    second = jnp.einsum(
        "ykbz,ybwm->wkmz",
        rotated,
        complex_table(inner_size, inner_size, inner_size, -1.0),
        precision=HIGHEST,
    )
    return second.reshape(2, seq_rows, item_width)


def local_inverse(columns, block_size):
    seq_rows = columns.shape[1]
    item_width = columns.shape[2]
    inner_size = seq_rows // block_size
    shaped = columns.reshape(2, block_size, inner_size, item_width)
    first_pass = jnp.einsum(
        "xkmz,xmyb->ykbz",
        shaped,
        complex_table(inner_size, inner_size, inner_size, 1.0),
        precision=HIGHEST,
    )
    cosine, sine_part = block_angles(block_size, inner_size, seq_rows, 1.0)
    rotated = rotate(first_pass, cosine, sine_part)
    second = jnp.einsum(
        "xkbz,xkya->yabz",
        rotated,
        complex_table(block_size, block_size, block_size, 1.0),
        precision=HIGHEST,
    )
    return second.reshape(2, seq_rows, item_width) * (1.0 / seq_rows)


def cross_transform(columns, dft_table):
    seq_rows = columns.shape[1]
    item_width = columns.shape[2]
    shaped = columns.reshape(2, 1, seq_rows, item_width)
    transformed = jnp.einsum(
        "xpjz,xpyk->ykjz",
        lax.all_to_all(shaped, "seq", split_axis=2, concat_axis=1, tiled=True),
        dft_table,
        precision=HIGHEST,
    )
    result = lax.all_to_all(transformed, "seq", split_axis=1, concat_axis=2, tiled=True)
    return result.reshape(2, seq_rows, item_width)


def shard_twiddle(columns, frequency, seq_length, direction):
    seq_rows = columns.shape[1]
    local_pos = jnp.arange(seq_rows, dtype=jnp.int32)
    rotation = (
        direction
        * 2.0
        * math.pi
        / seq_length
        * (local_pos * frequency % seq_length).astype(jnp.float32)
    )
    return rotate(columns, jnp.cos(rotation)[:, None], jnp.sin(rotation)[:, None])


def forward(columns, shard_index, devices, block_size):
    seq_length = columns.shape[1] * devices
    columns = cross_transform(columns, complex_table(devices, devices, devices, -1.0))
    columns = shard_twiddle(columns, shard_index, seq_length, -1.0)
    return local_forward(columns, block_size)


def inverse(columns, shard_index, devices, block_size):
    seq_length = columns.shape[1] * devices
    columns = local_inverse(columns, block_size)
    columns = shard_twiddle(columns, shard_index, seq_length, 1.0)
    columns = cross_transform(
        columns, complex_table(devices, devices, devices, 1.0) * (1.0 / devices)
    )
    return columns


def per_device(inputs, value_weight, query_weight, filters, grad_out):
    channel_count = filters.shape[0]
    seq_rows = filters.shape[1]
    devices = lax.axis_size("seq")
    shard_index = lax.axis_index("seq")
    seq_length = seq_rows * devices
    grad_scale = 1.0 / math.sqrt(seq_length)
    all_inputs = lax.all_gather(inputs, "chan", axis=0, tiled=True)
    projected = jnp.einsum("cd,ct->dt", value_weight, all_inputs, precision=HIGHEST)
    query_proj = jnp.einsum("cd,ct->dt", query_weight, all_inputs, precision=HIGHEST)
    gated_grad = grad_out * query_proj
    signals = jnp.stack([projected, filters, gated_grad])
    position = shard_index * seq_rows + jnp.arange(seq_rows, dtype=jnp.int32)
    twist_angle = 0.5 * math.pi / seq_length * position.astype(jnp.float32)
    cosine = jnp.cos(twist_angle)
    sine_part = jnp.sin(twist_angle)
    twisted = jnp.stack([signals * cosine, -signals * sine_part])
    columns = jnp.transpose(twisted, (0, 3, 1, 2)).reshape(2, seq_rows, 3 * channel_count)
    spectra = forward(columns, shard_index, devices, BLK).reshape(2, seq_rows, 3, channel_count)
    value_spec = spectra[:, :, 0]
    filter_spec = spectra[:, :, 1]
    grad_spec = spectra[:, :, 2]
    products = jnp.stack(
        [
            multiply(filter_spec, value_spec, False),
            multiply(filter_spec, grad_spec, True),
            multiply(value_spec, grad_spec, True),
        ],
        axis=2,
    )
    restored = inverse(
        products.reshape(2, seq_rows, 3 * channel_count), shard_index, devices, BLK
    ).reshape(2, seq_rows, 3, channel_count)
    combined = restored[0] * cosine[:, None, None] - restored[1] * sine_part[:, None, None]
    combined = jnp.transpose(combined, (1, 2, 0))
    convolved = combined[0]
    grad_value = combined[1]
    filter_grad = combined[2] * grad_scale
    grad_query = grad_out * convolved
    input_grad = lax.psum_scatter(
        jnp.dot(value_weight, grad_value, precision=HIGHEST, preferred_element_type=jnp.float32)
        + jnp.dot(query_weight, grad_query, precision=HIGHEST, preferred_element_type=jnp.float32),
        "chan",
        scatter_dimension=0,
        tiled=True,
    )
    partial_value = jnp.einsum("ct,dt->cd", all_inputs, grad_value, precision=HIGHEST) * grad_scale
    partial_query = jnp.einsum("ct,dt->cd", all_inputs, grad_query, precision=HIGHEST) * grad_scale
    value_gradient, query_gradient = lax.psum((partial_value, partial_query), "seq")
    return (input_grad, filter_grad, value_gradient, query_gradient)


NN = (((1,), (0,)), ((), ()))
NT = (((1,), (1,)), ((), ()))


def split_table(table):
    high = table.astype(jnp.bfloat16)
    low = (table - high.astype(np.float32)).astype(jnp.bfloat16)
    return high, low


@functools.lru_cache(maxsize=None)
def transform_tables(seq_length):
    outer = seq_length // LANES
    k = np.arange(outer, dtype=np.float64)
    a = np.arange(outer, dtype=np.float64)
    b = np.arange(LANES, dtype=np.float64)
    phase = 2 * np.pi * np.outer(4 * k + 1, a) % (2 * np.pi * 4 * outer) / (4 * outer)
    small = np.concatenate([np.cos(phase), -np.sin(phase)], axis=0)
    wide = np.repeat(small, GROUP, axis=0).astype(np.float32)
    tall = (np.repeat(small.T, GROUP, axis=0) / seq_length).astype(np.float32)
    angle = 2 * np.pi * np.repeat(np.outer(4 * k + 1, b), GROUP, axis=0) / (4 * seq_length)
    turn = np.stack([np.cos(angle), np.sin(angle)]).astype(np.float32)
    inner = 2 * np.pi * (np.outer(b, b) % LANES) / LANES
    c, s = np.cos(inner), np.sin(inner)
    ahead = np.block([[c, -s], [s, c]]).astype(np.float32)
    back = np.block([[c, s], [-s, c]]).astype(np.float32)
    return (
        *split_table(wide),
        *split_table(tall),
        *split_table(ahead),
        *split_table(back),
        turn,
    )


def split(x):
    high = x.astype(jnp.bfloat16)
    return high, (x - high.astype(jnp.float32)).astype(jnp.bfloat16)


def dot3(first, second, dims=NN):
    def dot(x, y):
        return lax.dot_general(x, y, dims, preferred_element_type=jnp.float32)

    return dot(first[0], second[0]) + (dot(first[0], second[1]) + dot(first[1], second[0]))


def spread(small_ref, out_ref):
    rows, cols = out_ref.shape
    inner = small_ref.shape[1]
    pick = lax.broadcasted_iota(jnp.int32, (inner, cols), 1) // GROUP
    own = lax.broadcasted_iota(jnp.int32, (inner, cols), 0)
    picks = jnp.where(pick == own, 1.0, 0.0).astype(jnp.bfloat16)
    row_lane = lax.broadcasted_iota(jnp.int32, (rows, cols), 0) % GROUP
    col_lane = lax.broadcasted_iota(jnp.int32, (rows, cols), 1) % GROUP
    full = lax.dot_general(small_ref[...], picks, NN, preferred_element_type=jnp.float32)
    out_ref[...] = jnp.where(row_lane == col_lane, full, 0.0).astype(jnp.bfloat16)


def fused_kernel(devices, scale, *refs):
    x_hbm, vw_hbm, qw_hbm, f_hbm, g_hbm = refs[:5]
    table_hbm = refs[5:14]
    ig_out, fg_out, vg_out, qg_out = refs[14:18]
    x_ref, vw_ref, qw_ref, g_ref = refs[18:22]
    small_refs = refs[22:26]
    ahead_h, ahead_l, back_h, back_l, turn_ref = refs[26:31]
    wide_h, wide_l, tall_h, tall_l = refs[31:35]
    other_x, send_sig, in_sig, spec, out_sig, ret_sig, part, scat, red, gath = refs[35:45]
    ig_send, ig_recv, ssem, rsem, csend, crecv, lsem, osem = refs[45:]
    me = lax.axis_index("seq")
    chan = lax.axis_index("chan")
    half, width = x_ref.shape
    pieces = width // LANES
    rows = 2 * half // devices

    def peer_of(i):
        peer, bit = me, 1
        while bit < devices:
            peer = peer + (i // bit) % 2 * (1 - 2 * (me // bit % 2)) * bit
            bit *= 2
        return peer

    barrier = pltpu.get_barrier_semaphore()

    def greet(i, carry):
        pl.semaphore_signal(
            barrier,
            inc=1,
            device_id={"seq": peer_of(devices - i)},
            device_id_type=pl.DeviceIdType.MESH,
        )
        return carry

    lax.fori_loop(1, devices, greet, 0)
    pl.semaphore_signal(
        barrier, inc=1, device_id={"chan": 1 - chan}, device_id_type=pl.DeviceIdType.MESH
    )

    loads = [
        pltpu.make_async_copy(src, dst, lsem.at[at])
        for at, (src, dst) in enumerate(
            zip(
                (x_hbm, vw_hbm, qw_hbm, g_hbm, *table_hbm),
                (x_ref, vw_ref, qw_ref, g_ref, *small_refs)
                + (ahead_h, ahead_l, back_h, back_l, turn_ref),
            )
        )
    ]
    for load in loads:
        load.start()
    own_f = pl.ds(pl.multiple_of(me * GROUP, GROUP), GROUP)
    keep_f = pltpu.make_async_copy(f_hbm.at[own_f, :], in_sig.at[0, me], lsem.at[len(loads)])
    keep_f.start()
    for load in loads[:3]:
        load.wait()

    own_rows = pl.ds(pl.multiple_of(chan * half, half), half)
    other_rows = pl.ds(pl.multiple_of((1 - chan) * half, half), half)
    own_x = split(x_ref[...])
    partial_value = dot3(split(vw_ref[own_rows, :].T), own_x)
    partial_query = dot3(split(qw_ref[own_rows, :].T), own_x)

    pl.semaphore_wait(barrier, devices)

    def exchange(index, src, dst):
        return pltpu.make_async_remote_copy(
            src_ref=src,
            dst_ref=dst,
            send_sem=csend.at[index],
            recv_sem=crecv.at[index],
            device_id={"chan": 1 - chan},
            device_id_type=pl.DeviceIdType.MESH,
        )

    def each(slot, src_of, dst_of, what):
        def step(i, carry):
            index = devices - i
            peer = peer_of(index)
            copy = pltpu.make_async_remote_copy(
                src_ref=src_of(peer),
                dst_ref=dst_of(),
                send_sem=ssem.at[slot, index],
                recv_sem=rsem.at[slot, index],
                device_id={"seq": peer},
                device_id_type=pl.DeviceIdType.MESH,
            )
            getattr(copy, what)()
            return carry

        lax.fori_loop(1, devices, step, 0)

    def group_rows(peer, count):
        return pl.ds(pl.multiple_of(peer * count, count), count)

    def out_way(slot, what):
        src = f_hbm if slot == 0 else send_sig.at[slot - 1]
        each(slot, lambda p: src.at[group_rows(p, GROUP), :], lambda: in_sig.at[slot, me], what)

    def back_way(slot, what):
        each(
            3 + slot,
            lambda p: out_sig.at[slot, p],
            lambda: ret_sig.at[slot, group_rows(me, GROUP), :],
            what,
        )

    def scatter(slot, what):
        each(
            6 + slot,
            lambda p: part.at[slot, group_rows(p, rows), :],
            lambda: scat.at[slot, me],
            what,
        )

    def gather(slot, what):
        each(
            8 + slot,
            lambda p: red.at[slot],
            lambda: gath.at[slot, group_rows(me, rows), :],
            what,
        )

    give_x = exchange(0, x_hbm, other_x)
    give_x.start()
    out_way(0, "start")
    give_x.wait()

    far_x = split(other_x[...])
    send_sig[0] = partial_value + dot3(split(vw_ref[other_rows, :].T), far_x)
    out_way(1, "start")
    in_sig[1, me] = send_sig[0, group_rows(me, GROUP), :]
    query_proj = partial_query + dot3(split(qw_ref[other_rows, :].T), far_x)
    loads[3].wait()
    send_sig[1] = g_ref[...] * query_proj
    out_way(2, "start")
    in_sig[2, me] = send_sig[1, group_rows(me, GROUP), :]

    for load in loads[4:]:
        load.wait()
    for small_ref, out_ref in zip(small_refs, (wide_h, wide_l, tall_h, tall_l)):
        spread(small_ref, out_ref)
    keep_f.wait()
    wide = (wide_h[...], wide_l[...])
    tall = (tall_h[...], tall_l[...])
    ahead = (ahead_h[...], ahead_l[...])
    back = (back_h[...], back_l[...])
    cosine = turn_ref[0]
    sine = turn_ref[1]
    count = cosine.shape[0]

    def transform(slot):
        signal = jnp.concatenate(
            [
                in_sig[slot, source, :, piece * LANES : (piece + 1) * LANES]
                for source in range(devices)
                for piece in range(pieces)
            ],
            axis=0,
        )
        first = dot3(wide, split(signal))
        real, imag = first[:count], first[count:]
        turned = jnp.concatenate(
            [real * cosine + imag * sine, imag * cosine - real * sine], axis=1
        )
        spec[slot] = dot3(split(turned), ahead)

    def restore(first, second, conjugate, slot):
        real_a, imag_a = spec[first, :, :LANES], spec[first, :, LANES:]
        real_b, imag_b = spec[second, :, :LANES], spec[second, :, LANES:]
        if conjugate:
            imag_a = -imag_a
        product = jnp.concatenate(
            [real_a * real_b - imag_a * imag_b, real_a * imag_b + imag_a * real_b], axis=1
        )
        inner = dot3(split(product), back)
        real, imag = inner[:, :LANES], inner[:, LANES:]
        turned = jnp.concatenate(
            [real * cosine - imag * sine, imag * cosine + real * sine], axis=0
        )
        signal = dot3(tall, split(turned))
        if slot == 2:
            signal = signal * scale
        for target in range(devices):
            for piece in range(pieces):
                at = (target * pieces + piece) * GROUP
                out_sig[slot, target, :, piece * LANES : (piece + 1) * LANES] = signal[
                    at : at + GROUP
                ]
        back_way(slot, "start")
        ret_sig[slot, group_rows(me, GROUP), :] = out_sig[slot, me]

    out_way(0, "wait_recv")
    transform(0)
    out_way(1, "wait_recv")
    transform(1)
    restore(0, 1, False, 0)
    out_way(2, "wait_recv")
    transform(2)
    restore(0, 2, True, 1)
    restore(1, 2, True, 2)

    def weight_part(slot, grad):
        near = dot3(own_x2, grad, NT)
        far = dot3(far_x2, grad, NT)
        part[slot, own_rows, :] = near
        part[slot, other_rows, :] = far
        scatter(slot, "start")
        scat[slot, me] = part[slot, group_rows(me, rows), :]

    own_x2 = split(x_ref[...])
    far_x2 = split(other_x[...])
    back_way(0, "wait_recv")
    grad_query = split(g_ref[...] * ret_sig[0])
    weight_part(0, grad_query)
    near_grad = dot3(split(qw_ref[own_rows, :]), grad_query)
    far_grad = dot3(split(qw_ref[other_rows, :]), grad_query)
    back_way(1, "wait_recv")
    grad_value = split(ret_sig[1])
    ig_send[...] = far_grad + dot3(split(vw_ref[other_rows, :]), grad_value)
    give_ig = exchange(1, ig_send, ig_recv)
    give_ig.start()
    weight_part(1, grad_value)

    def reduce(slot):
        scatter(slot, "wait_recv")
        total = scat[slot, 0]
        for source in range(1, devices):
            total = total + scat[slot, source]
        red[slot] = total * scale
        gather(slot, "start")
        gath[slot, group_rows(me, rows), :] = red[slot]

    reduce(0)
    near_grad = near_grad + dot3(split(vw_ref[own_rows, :]), grad_value)
    reduce(1)
    give_ig.wait()
    ig_recv[...] = near_grad + ig_recv[...]
    stores = [pltpu.make_async_copy(ig_recv, ig_out, osem.at[0])]
    stores[0].start()
    back_way(2, "wait_recv")
    stores.append(pltpu.make_async_copy(ret_sig.at[2], fg_out, osem.at[1]))
    stores[1].start()
    for slot, out in ((0, qg_out), (1, vg_out)):
        gather(slot, "wait_recv")
        stores.append(pltpu.make_async_copy(gath.at[slot], out, osem.at[2 + slot]))
        stores[-1].start()
    for slot in range(3):
        out_way(slot, "wait_send")
        back_way(slot, "wait_send")
    for slot in range(2):
        scatter(slot, "wait_send")
        gather(slot, "wait_send")
    for store in stores:
        store.wait()


def finish_kernel(*refs):
    for source, target in zip(refs[:4], refs[4:]):
        target[...] = source[...]


def fused_device(inputs, value_weight, query_weight, filters, grad_out):
    half, width = inputs.shape
    devices = lax.axis_size("seq")
    seq_length = width * devices
    depth = value_weight.shape[0]
    rows = depth // devices
    tables = transform_tables(seq_length)
    count = seq_length // LANES * GROUP
    tables = [jnp.asarray(t) for t in tables]
    hbm = pl.BlockSpec(memory_space=pl.ANY)
    vmem = pl.BlockSpec(memory_space=pltpu.VMEM)
    f32, bf16 = jnp.float32, jnp.bfloat16
    outs = (
        jax.ShapeDtypeStruct((half, width), f32),
        jax.ShapeDtypeStruct((half, width), f32),
        jax.ShapeDtypeStruct((depth, half), f32),
        jax.ShapeDtypeStruct((depth, half), f32),
    )
    results = pl.pallas_call(
        functools.partial(fused_kernel, devices, 1.0 / math.sqrt(seq_length)),
        out_shape=outs,
        in_specs=[hbm] * (5 + len(tables)),
        out_specs=(hbm,) * 4,
        scratch_shapes=[
            pltpu.VMEM((half, width), f32),
            pltpu.VMEM((depth, half), f32),
            pltpu.VMEM((depth, half), f32),
            pltpu.VMEM((half, width), f32),
            *(pltpu.VMEM(t.shape, t.dtype) for t in tables),
            pltpu.VMEM((2 * count, count), bf16),
            pltpu.VMEM((2 * count, count), bf16),
            pltpu.VMEM((count, 2 * count), bf16),
            pltpu.VMEM((count, 2 * count), bf16),
            pltpu.VMEM((half, width), f32),
            pltpu.VMEM((2, half, width), f32),
            pltpu.VMEM((3, devices, GROUP, width), f32),
            pltpu.VMEM((3, count, 2 * LANES), f32),
            pltpu.VMEM((3, devices, GROUP, width), f32),
            pltpu.VMEM((3, half, width), f32),
            pltpu.VMEM((2, depth, half), f32),
            pltpu.VMEM((2, devices, rows, half), f32),
            pltpu.VMEM((2, rows, half), f32),
            pltpu.VMEM((2, depth, half), f32),
            pltpu.VMEM((half, width), f32),
            pltpu.VMEM((half, width), f32),
            pltpu.SemaphoreType.DMA((10, devices)),
            pltpu.SemaphoreType.DMA((10, devices)),
            pltpu.SemaphoreType.DMA((2,)),
            pltpu.SemaphoreType.DMA((2,)),
            pltpu.SemaphoreType.DMA((5 + len(tables),)),
            pltpu.SemaphoreType.DMA((4,)),
        ],
        compiler_params=pltpu.CompilerParams(
            collective_id=0, has_side_effects=True, vmem_limit_bytes=60 * 1024 * 1024
        ),
    )(inputs, value_weight, query_weight, filters, grad_out, *tables)
    return tuple(
        pl.pallas_call(
            finish_kernel, out_shape=outs, in_specs=[vmem] * 4, out_specs=(vmem,) * 4
        )(*results)
    )


def on_device(inputs, value_weight, query_weight, filters, grad_out):
    channel_count, width = filters.shape
    devices = lax.axis_size("seq")
    fits = (
        channel_count == GROUP * devices
        and channel_count == inputs.shape[0]
        and lax.axis_size("chan") == 2
        and width % LANES == 0
        and channel_count % LANES == 0
        and devices & (devices - 1) == 0
        and value_weight.shape[0] % (GROUP * devices) == 0
    )
    body = fused_device if fits else per_device
    return body(inputs, value_weight, query_weight, filters, grad_out)


def solution(mesh):
    return jax.shard_map(
        on_device,
        mesh=mesh,
        in_specs=(
            P("chan", "seq"),
            P(None, "chan"),
            P(None, "chan"),
            P("chan", "seq"),
            P("chan", "seq"),
        ),
        out_specs=(P("chan", "seq"), P("chan", "seq"), P(None, "chan"), P(None, "chan")),
        check_vma=False,
    )
```

```python
import functools
import math

import jax
import jax.numpy as jnp
import numpy as np
from jax import lax
from jax.experimental import pallas as pl
from jax.experimental.pallas import tpu as pltpu
from jax.sharding import PartitionSpec as P

BLK = 64
LANES = 128
GROUP = 8


HIGHEST = lax.Precision.HIGHEST


def complex_table(row_count, col_count, period, direction):
    row_iota = lax.broadcasted_iota(jnp.int32, (row_count, col_count), 0)
    col_iota = lax.broadcasted_iota(jnp.int32, (row_count, col_count), 1)
    rotation = 2.0 * math.pi / period * (row_iota * col_iota % period).astype(jnp.float32)
    cosine = jnp.cos(rotation)
    sine_part = direction * jnp.sin(rotation)
    upper_rows = jnp.stack([cosine, sine_part], axis=1)
    lower_rows = jnp.stack([-sine_part, cosine], axis=1)
    return jnp.stack([upper_rows, lower_rows], axis=0)


def rotate(columns, cosine, sine_part):
    return jnp.stack(
        [columns[0] * cosine - columns[1] * sine_part, columns[0] * sine_part + columns[1] * cosine]
    )


def multiply(first_spec, second_spec, conjugate):
    imag_first = -first_spec[1] if conjugate else first_spec[1]
    return jnp.stack(
        [
            first_spec[0] * second_spec[0] - imag_first * second_spec[1],
            first_spec[0] * second_spec[1] + imag_first * second_spec[0],
        ]
    )


def block_angles(block_size, inner_size, seq_rows, direction):
    outer_iota = lax.broadcasted_iota(jnp.int32, (block_size, inner_size), 0)
    inner_iota = lax.broadcasted_iota(jnp.int32, (block_size, inner_size), 1)
    rotation = (
        direction
        * 2.0
        * math.pi
        / seq_rows
        * (outer_iota * inner_iota % seq_rows).astype(jnp.float32)
    )
    return (jnp.cos(rotation)[:, :, None], jnp.sin(rotation)[:, :, None])


def local_forward(columns, block_size):
    seq_rows = columns.shape[1]
    item_width = columns.shape[2]
    inner_size = seq_rows // block_size
    shaped = columns.reshape(2, block_size, inner_size, item_width)
    first_pass = jnp.einsum(
        "xabz,xayk->ykbz",
        shaped,
        complex_table(block_size, block_size, block_size, -1.0),
        precision=HIGHEST,
    )
    cosine, sine_part = block_angles(block_size, inner_size, seq_rows, -1.0)
    rotated = rotate(first_pass, cosine, sine_part)
    second = jnp.einsum(
        "ykbz,ybwm->wkmz",
        rotated,
        complex_table(inner_size, inner_size, inner_size, -1.0),
        precision=HIGHEST,
    )
    return second.reshape(2, seq_rows, item_width)


def local_inverse(columns, block_size):
    seq_rows = columns.shape[1]
    item_width = columns.shape[2]
    inner_size = seq_rows // block_size
    shaped = columns.reshape(2, block_size, inner_size, item_width)
    first_pass = jnp.einsum(
        "xkmz,xmyb->ykbz",
        shaped,
        complex_table(inner_size, inner_size, inner_size, 1.0),
        precision=HIGHEST,
    )
    cosine, sine_part = block_angles(block_size, inner_size, seq_rows, 1.0)
    rotated = rotate(first_pass, cosine, sine_part)
    second = jnp.einsum(
        "xkbz,xkya->yabz",
        rotated,
        complex_table(block_size, block_size, block_size, 1.0),
        precision=HIGHEST,
    )
    return second.reshape(2, seq_rows, item_width) * (1.0 / seq_rows)


def cross_transform(columns, dft_table):
    seq_rows = columns.shape[1]
    item_width = columns.shape[2]
    shaped = columns.reshape(2, 1, seq_rows, item_width)
    transformed = jnp.einsum(
        "xpjz,xpyk->ykjz",
        lax.all_to_all(shaped, "seq", split_axis=2, concat_axis=1, tiled=True),
        dft_table,
        precision=HIGHEST,
    )
    result = lax.all_to_all(transformed, "seq", split_axis=1, concat_axis=2, tiled=True)
    return result.reshape(2, seq_rows, item_width)


def shard_twiddle(columns, frequency, seq_length, direction):
    seq_rows = columns.shape[1]
    local_pos = jnp.arange(seq_rows, dtype=jnp.int32)
    rotation = (
        direction
        * 2.0
        * math.pi
        / seq_length
        * (local_pos * frequency % seq_length).astype(jnp.float32)
    )
    return rotate(columns, jnp.cos(rotation)[:, None], jnp.sin(rotation)[:, None])


def forward(columns, shard_index, devices, block_size):
    seq_length = columns.shape[1] * devices
    columns = cross_transform(columns, complex_table(devices, devices, devices, -1.0))
    columns = shard_twiddle(columns, shard_index, seq_length, -1.0)
    return local_forward(columns, block_size)


def inverse(columns, shard_index, devices, block_size):
    seq_length = columns.shape[1] * devices
    columns = local_inverse(columns, block_size)
    columns = shard_twiddle(columns, shard_index, seq_length, 1.0)
    columns = cross_transform(
        columns, complex_table(devices, devices, devices, 1.0) * (1.0 / devices)
    )
    return columns


def per_device(inputs, value_weight, query_weight, filters, grad_out):
    channel_count = filters.shape[0]
    seq_rows = filters.shape[1]
    devices = lax.axis_size("seq")
    shard_index = lax.axis_index("seq")
    seq_length = seq_rows * devices
    grad_scale = 1.0 / math.sqrt(seq_length)
    all_inputs = lax.all_gather(inputs, "chan", axis=0, tiled=True)
    projected = jnp.einsum("cd,ct->dt", value_weight, all_inputs, precision=HIGHEST)
    query_proj = jnp.einsum("cd,ct->dt", query_weight, all_inputs, precision=HIGHEST)
    gated_grad = grad_out * query_proj
    signals = jnp.stack([projected, filters, gated_grad])
    position = shard_index * seq_rows + jnp.arange(seq_rows, dtype=jnp.int32)
    twist_angle = 0.5 * math.pi / seq_length * position.astype(jnp.float32)
    cosine = jnp.cos(twist_angle)
    sine_part = jnp.sin(twist_angle)
    twisted = jnp.stack([signals * cosine, -signals * sine_part])
    columns = jnp.transpose(twisted, (0, 3, 1, 2)).reshape(2, seq_rows, 3 * channel_count)
    spectra = forward(columns, shard_index, devices, BLK).reshape(2, seq_rows, 3, channel_count)
    value_spec = spectra[:, :, 0]
    filter_spec = spectra[:, :, 1]
    grad_spec = spectra[:, :, 2]
    products = jnp.stack(
        [
            multiply(filter_spec, value_spec, False),
            multiply(filter_spec, grad_spec, True),
            multiply(value_spec, grad_spec, True),
        ],
        axis=2,
    )
    restored = inverse(
        products.reshape(2, seq_rows, 3 * channel_count), shard_index, devices, BLK
    ).reshape(2, seq_rows, 3, channel_count)
    combined = restored[0] * cosine[:, None, None] - restored[1] * sine_part[:, None, None]
    combined = jnp.transpose(combined, (1, 2, 0))
    convolved = combined[0]
    grad_value = combined[1]
    filter_grad = combined[2] * grad_scale
    grad_query = grad_out * convolved
    input_grad = lax.psum_scatter(
        jnp.dot(value_weight, grad_value, precision=HIGHEST, preferred_element_type=jnp.float32)
        + jnp.dot(query_weight, grad_query, precision=HIGHEST, preferred_element_type=jnp.float32),
        "chan",
        scatter_dimension=0,
        tiled=True,
    )
    partial_value = jnp.einsum("ct,dt->cd", all_inputs, grad_value, precision=HIGHEST) * grad_scale
    partial_query = jnp.einsum("ct,dt->cd", all_inputs, grad_query, precision=HIGHEST) * grad_scale
    value_gradient, query_gradient = lax.psum((partial_value, partial_query), "seq")
    return (input_grad, filter_grad, value_gradient, query_gradient)


NN = (((1,), (0,)), ((), ()))
NT = (((1,), (1,)), ((), ()))


def split_table(table):
    high = table.astype(jnp.bfloat16)
    low = (table - high.astype(np.float32)).astype(jnp.bfloat16)
    return high, low


@functools.lru_cache(maxsize=None)
def transform_tables(seq_length):
    outer = seq_length // LANES
    k = np.arange(outer, dtype=np.float64)
    a = np.arange(outer, dtype=np.float64)
    b = np.arange(LANES, dtype=np.float64)
    phase = 2 * np.pi * np.outer(4 * k + 1, a) % (2 * np.pi * 4 * outer) / (4 * outer)
    small = np.concatenate([np.cos(phase), -np.sin(phase)], axis=0)
    wide = np.repeat(small, GROUP, axis=0).astype(np.float32)
    tall = (np.repeat(small.T, GROUP, axis=0) / seq_length).astype(np.float32)
    angle = 2 * np.pi * np.repeat(np.outer(4 * k + 1, b), GROUP, axis=0) / (4 * seq_length)
    turn = np.stack([np.cos(angle), np.sin(angle)]).astype(np.float32)
    inner = 2 * np.pi * (np.outer(b, b) % LANES) / LANES
    c, s = np.cos(inner), np.sin(inner)
    ahead = np.block([[c, -s], [s, c]]).astype(np.float32)
    back = np.block([[c, s], [-s, c]]).astype(np.float32)
    return (
        *split_table(wide),
        *split_table(tall),
        *split_table(ahead),
        *split_table(back),
        turn,
    )


def split(x):
    high = x.astype(jnp.bfloat16)
    return high, (x - high.astype(jnp.float32)).astype(jnp.bfloat16)


def dot3(first, second, dims=NN):
    def dot(x, y):
        return lax.dot_general(x, y, dims, preferred_element_type=jnp.float32)

    return dot(first[0], second[0]) + (dot(first[0], second[1]) + dot(first[1], second[0]))


def spread(small_ref, out_ref):
    rows, cols = out_ref.shape
    inner = small_ref.shape[1]
    pick = lax.broadcasted_iota(jnp.int32, (inner, cols), 1) // GROUP
    own = lax.broadcasted_iota(jnp.int32, (inner, cols), 0)
    picks = jnp.where(pick == own, 1.0, 0.0).astype(jnp.bfloat16)
    row_lane = lax.broadcasted_iota(jnp.int32, (rows, cols), 0) % GROUP
    col_lane = lax.broadcasted_iota(jnp.int32, (rows, cols), 1) % GROUP
    full = lax.dot_general(small_ref[...], picks, NN, preferred_element_type=jnp.float32)
    out_ref[...] = jnp.where(row_lane == col_lane, full, 0.0).astype(jnp.bfloat16)


def fused_kernel(devices, scale, *refs):
    x_hbm, vw_hbm, qw_hbm, f_hbm, g_hbm = refs[:5]
    table_hbm = refs[5:14]
    ig_out, fg_out, vg_out, qg_out = refs[14:18]
    x_ref, vw_ref, qw_ref, g_ref = refs[18:22]
    small_refs = refs[22:26]
    ahead_h, ahead_l, back_h, back_l, turn_ref = refs[26:31]
    wide_h, wide_l, tall_h, tall_l = refs[31:35]
    other_x, send_sig, in_sig, spec, out_sig, ret_sig, part, scat, red, gath = refs[35:45]
    ig_send, ig_recv, ssem, rsem, csend, crecv, lsem, osem = refs[45:]
    me = lax.axis_index("seq")
    chan = lax.axis_index("chan")
    half, width = x_ref.shape
    pieces = width // LANES
    inner = 1 << (devices.bit_length() - 1) // 2
    outer = devices // inner
    rows = 2 * half // inner
    me_inner, me_outer = me % inner, me // inner

    def peer_of(i):
        peer, bit = me, 1
        while bit < devices:
            peer = peer + (i // bit) % 2 * (1 - 2 * (me // bit % 2)) * bit
            bit *= 2
        return peer

    barrier = pltpu.get_barrier_semaphore()

    def greet(i, carry):
        pl.semaphore_signal(
            barrier,
            inc=1,
            device_id={"seq": peer_of(devices - i)},
            device_id_type=pl.DeviceIdType.MESH,
        )
        return carry

    lax.fori_loop(1, devices, greet, 0)
    pl.semaphore_signal(
        barrier, inc=1, device_id={"chan": 1 - chan}, device_id_type=pl.DeviceIdType.MESH
    )

    loads = [
        pltpu.make_async_copy(src, dst, lsem.at[at])
        for at, (src, dst) in enumerate(
            zip(
                (x_hbm, vw_hbm, qw_hbm, g_hbm, *table_hbm),
                (x_ref, vw_ref, qw_ref, g_ref, *small_refs)
                + (ahead_h, ahead_l, back_h, back_l, turn_ref),
            )
        )
    ]
    for load in loads:
        load.start()
    own_f = pl.ds(pl.multiple_of(me * GROUP, GROUP), GROUP)
    keep_f = pltpu.make_async_copy(f_hbm.at[own_f, :], in_sig.at[0, me], lsem.at[len(loads)])
    keep_f.start()
    for load in loads[:3]:
        load.wait()

    own_rows = pl.ds(pl.multiple_of(chan * half, half), half)
    other_rows = pl.ds(pl.multiple_of((1 - chan) * half, half), half)
    own_x = split(x_ref[...])
    partial_value = dot3(split(vw_ref[own_rows, :].T), own_x)
    partial_query = dot3(split(qw_ref[own_rows, :].T), own_x)

    pl.semaphore_wait(barrier, devices)

    def exchange(index, src, dst):
        return pltpu.make_async_remote_copy(
            src_ref=src,
            dst_ref=dst,
            send_sem=csend.at[index],
            recv_sem=crecv.at[index],
            device_id={"chan": 1 - chan},
            device_id_type=pl.DeviceIdType.MESH,
        )

    def each(slot, src_of, dst_of, what, count=devices, stride=1):
        def step(i, carry):
            index = (count - i) * stride
            peer = peer_of(index)
            copy = pltpu.make_async_remote_copy(
                src_ref=src_of(peer),
                dst_ref=dst_of(),
                send_sem=ssem.at[slot, index],
                recv_sem=rsem.at[slot, index],
                device_id={"seq": peer},
                device_id_type=pl.DeviceIdType.MESH,
            )
            getattr(copy, what)()
            return carry

        lax.fori_loop(1, count, step, 0)

    def group_rows(peer, count):
        return pl.ds(pl.multiple_of(peer * count, count), count)

    def out_way(slot, what):
        src = f_hbm if slot == 0 else send_sig.at[slot - 1]
        each(slot, lambda p: src.at[group_rows(p, GROUP), :], lambda: in_sig.at[slot, me], what)

    def back_way(slot, what):
        each(
            3 + slot,
            lambda p: out_sig.at[slot, p],
            lambda: ret_sig.at[slot, group_rows(me, GROUP), :],
            what,
        )

    def scatter(slot, what):
        each(
            6 + slot,
            lambda p: part.at[slot, group_rows(p % inner, rows), :],
            lambda: scat.at[slot, me_inner],
            what,
            inner,
        )

    def swap(slot, what):
        each(
            8 + slot,
            lambda p: red.at[slot, me_outer],
            lambda: red.at[slot, me_outer],
            what,
            outer,
            inner,
        )

    def gather(slot, what):
        each(
            10 + slot,
            lambda p: gath.at[slot, group_rows(me_inner, rows), :],
            lambda: gath.at[slot, group_rows(me_inner, rows), :],
            what,
            inner,
        )

    give_x = exchange(0, x_hbm, other_x)
    give_x.start()
    out_way(0, "start")
    give_x.wait()

    far_x = split(other_x[...])
    send_sig[0] = partial_value + dot3(split(vw_ref[other_rows, :].T), far_x)
    out_way(1, "start")
    in_sig[1, me] = send_sig[0, group_rows(me, GROUP), :]
    query_proj = partial_query + dot3(split(qw_ref[other_rows, :].T), far_x)
    loads[3].wait()
    send_sig[1] = g_ref[...] * query_proj
    out_way(2, "start")
    in_sig[2, me] = send_sig[1, group_rows(me, GROUP), :]

    for load in loads[4:]:
        load.wait()
    for small_ref, out_ref in zip(small_refs, (wide_h, wide_l, tall_h, tall_l)):
        spread(small_ref, out_ref)
    keep_f.wait()
    wide = (wide_h[...], wide_l[...])
    tall = (tall_h[...], tall_l[...])
    ahead = (ahead_h[...], ahead_l[...])
    back = (back_h[...], back_l[...])
    cosine = turn_ref[0]
    sine = turn_ref[1]
    count = cosine.shape[0]

    def transform(slot):
        signal = jnp.concatenate(
            [
                in_sig[slot, source, :, piece * LANES : (piece + 1) * LANES]
                for source in range(devices)
                for piece in range(pieces)
            ],
            axis=0,
        )
        first = dot3(wide, split(signal))
        real, imag = first[:count], first[count:]
        turned = jnp.concatenate(
            [real * cosine + imag * sine, imag * cosine - real * sine], axis=1
        )
        spec[slot] = dot3(split(turned), ahead)

    def restore(first, second, conjugate, slot):
        real_a, imag_a = spec[first, :, :LANES], spec[first, :, LANES:]
        real_b, imag_b = spec[second, :, :LANES], spec[second, :, LANES:]
        if conjugate:
            imag_a = -imag_a
        product = jnp.concatenate(
            [real_a * real_b - imag_a * imag_b, real_a * imag_b + imag_a * real_b], axis=1
        )
        inner = dot3(split(product), back)
        real, imag = inner[:, :LANES], inner[:, LANES:]
        turned = jnp.concatenate(
            [real * cosine - imag * sine, imag * cosine + real * sine], axis=0
        )
        signal = dot3(tall, split(turned))
        if slot == 2:
            signal = signal * scale
        for target in range(devices):
            for piece in range(pieces):
                at = (target * pieces + piece) * GROUP
                out_sig[slot, target, :, piece * LANES : (piece + 1) * LANES] = signal[
                    at : at + GROUP
                ]
        back_way(slot, "start")
        ret_sig[slot, group_rows(me, GROUP), :] = out_sig[slot, me]

    out_way(0, "wait_recv")
    transform(0)
    out_way(1, "wait_recv")
    transform(1)
    restore(0, 1, False, 0)
    out_way(2, "wait_recv")
    transform(2)
    restore(0, 2, True, 1)
    restore(1, 2, True, 2)

    def weight_part(slot, grad):
        part[slot, own_rows, :] = dot3(own_x2, grad, NT)
        part[slot, other_rows, :] = dot3(far_x2, grad, NT)
        scatter(slot, "start")
        scat[slot, me_inner] = part[slot, group_rows(me_inner, rows), :]

    own_x2 = split(x_ref[...])
    far_x2 = split(other_x[...])
    back_way(0, "wait_recv")
    grad_query = split(g_ref[...] * ret_sig[0])
    weight_part(0, grad_query)
    near_grad = dot3(split(qw_ref[own_rows, :]), grad_query)
    far_grad = dot3(split(qw_ref[other_rows, :]), grad_query)

    def reduce_inner(slot):
        scatter(slot, "wait_recv")
        total = scat[slot, 0]
        for source in range(1, inner):
            total = total + scat[slot, source]
        red[slot, me_outer] = total
        swap(slot, "start")

    def reduce_outer(slot):
        swap(slot, "wait_recv")
        total = red[slot, 0]
        for source in range(1, outer):
            total = total + red[slot, source]
        gath[slot, group_rows(me_inner, rows), :] = total * scale
        gather(slot, "start")

    reduce_inner(0)
    back_way(1, "wait_recv")
    grad_value = split(ret_sig[1])
    weight_part(1, grad_value)
    ig_send[...] = far_grad + dot3(split(vw_ref[other_rows, :]), grad_value)
    give_ig = exchange(1, ig_send, ig_recv)
    give_ig.start()
    reduce_inner(1)
    near_grad = near_grad + dot3(split(vw_ref[own_rows, :]), grad_value)
    reduce_outer(0)
    give_ig.wait()
    ig_recv[...] = near_grad + ig_recv[...]
    stores = [pltpu.make_async_copy(ig_recv, ig_out, osem.at[0])]
    stores[0].start()
    reduce_outer(1)
    back_way(2, "wait_recv")
    stores.append(pltpu.make_async_copy(ret_sig.at[2], fg_out, osem.at[1]))
    stores[1].start()
    for slot, out in ((0, qg_out), (1, vg_out)):
        gather(slot, "wait_recv")
        stores.append(pltpu.make_async_copy(gath.at[slot], out, osem.at[2 + slot]))
        stores[-1].start()
    for slot in range(3):
        out_way(slot, "wait_send")
        back_way(slot, "wait_send")
    for slot in range(2):
        scatter(slot, "wait_send")
        swap(slot, "wait_send")
        gather(slot, "wait_send")
    for store in stores:
        store.wait()


def finish_kernel(*refs):
    for source, target in zip(refs[:4], refs[4:]):
        target[...] = source[...]


def fused_device(inputs, value_weight, query_weight, filters, grad_out):
    half, width = inputs.shape
    devices = lax.axis_size("seq")
    seq_length = width * devices
    depth = value_weight.shape[0]
    inner = 1 << (devices.bit_length() - 1) // 2
    outer = devices // inner
    rows = depth // inner
    tables = transform_tables(seq_length)
    count = seq_length // LANES * GROUP
    tables = [jnp.asarray(t) for t in tables]
    hbm = pl.BlockSpec(memory_space=pl.ANY)
    vmem = pl.BlockSpec(memory_space=pltpu.VMEM)
    f32, bf16 = jnp.float32, jnp.bfloat16
    outs = (
        jax.ShapeDtypeStruct((half, width), f32),
        jax.ShapeDtypeStruct((half, width), f32),
        jax.ShapeDtypeStruct((depth, half), f32),
        jax.ShapeDtypeStruct((depth, half), f32),
    )
    results = pl.pallas_call(
        functools.partial(fused_kernel, devices, 1.0 / math.sqrt(seq_length)),
        out_shape=outs,
        in_specs=[hbm] * (5 + len(tables)),
        out_specs=(hbm,) * 4,
        scratch_shapes=[
            pltpu.VMEM((half, width), f32),
            pltpu.VMEM((depth, half), f32),
            pltpu.VMEM((depth, half), f32),
            pltpu.VMEM((half, width), f32),
            *(pltpu.VMEM(t.shape, t.dtype) for t in tables),
            pltpu.VMEM((2 * count, count), bf16),
            pltpu.VMEM((2 * count, count), bf16),
            pltpu.VMEM((count, 2 * count), bf16),
            pltpu.VMEM((count, 2 * count), bf16),
            pltpu.VMEM((half, width), f32),
            pltpu.VMEM((2, half, width), f32),
            pltpu.VMEM((3, devices, GROUP, width), f32),
            pltpu.VMEM((3, count, 2 * LANES), f32),
            pltpu.VMEM((3, devices, GROUP, width), f32),
            pltpu.VMEM((3, half, width), f32),
            pltpu.VMEM((2, depth, half), f32),
            pltpu.VMEM((2, inner, rows, half), f32),
            pltpu.VMEM((2, outer, rows, half), f32),
            pltpu.VMEM((2, depth, half), f32),
            pltpu.VMEM((half, width), f32),
            pltpu.VMEM((half, width), f32),
            pltpu.SemaphoreType.DMA((12, devices)),
            pltpu.SemaphoreType.DMA((12, devices)),
            pltpu.SemaphoreType.DMA((2,)),
            pltpu.SemaphoreType.DMA((2,)),
            pltpu.SemaphoreType.DMA((5 + len(tables),)),
            pltpu.SemaphoreType.DMA((4,)),
        ],
        compiler_params=pltpu.CompilerParams(
            collective_id=0, has_side_effects=True, vmem_limit_bytes=60 * 1024 * 1024
        ),
    )(inputs, value_weight, query_weight, filters, grad_out, *tables)
    return tuple(
        pl.pallas_call(
            finish_kernel, out_shape=outs, in_specs=[vmem] * 4, out_specs=(vmem,) * 4
        )(*results)
    )


def on_device(inputs, value_weight, query_weight, filters, grad_out):
    channel_count, width = filters.shape
    devices = lax.axis_size("seq")
    fits = (
        channel_count == GROUP * devices
        and channel_count == inputs.shape[0]
        and lax.axis_size("chan") == 2
        and width % LANES == 0
        and channel_count % LANES == 0
        and devices & (devices - 1) == 0
        and value_weight.shape[0] % (GROUP * devices) == 0
    )
    body = fused_device if fits else per_device
    return body(inputs, value_weight, query_weight, filters, grad_out)


def solution(mesh):
    return jax.shard_map(
        on_device,
        mesh=mesh,
        in_specs=(
            P("chan", "seq"),
            P(None, "chan"),
            P(None, "chan"),
            P("chan", "seq"),
            P("chan", "seq"),
        ),
        out_specs=(P("chan", "seq"), P("chan", "seq"), P(None, "chan"), P(None, "chan")),
        check_vma=False,
    )
```

```python
import functools
import math

import jax
import jax.numpy as jnp
import numpy as np
from jax import lax
from jax.experimental import pallas as pl
from jax.experimental.pallas import tpu as pltpu
from jax.sharding import PartitionSpec as P

BLK = 64
LANES = 128
GROUP = 8


HIGHEST = lax.Precision.HIGHEST


def complex_table(row_count, col_count, period, direction):
    row_iota = lax.broadcasted_iota(jnp.int32, (row_count, col_count), 0)
    col_iota = lax.broadcasted_iota(jnp.int32, (row_count, col_count), 1)
    rotation = 2.0 * math.pi / period * (row_iota * col_iota % period).astype(jnp.float32)
    cosine = jnp.cos(rotation)
    sine_part = direction * jnp.sin(rotation)
    upper_rows = jnp.stack([cosine, sine_part], axis=1)
    lower_rows = jnp.stack([-sine_part, cosine], axis=1)
    return jnp.stack([upper_rows, lower_rows], axis=0)


def rotate(columns, cosine, sine_part):
    return jnp.stack(
        [columns[0] * cosine - columns[1] * sine_part, columns[0] * sine_part + columns[1] * cosine]
    )


def multiply(first_spec, second_spec, conjugate):
    imag_first = -first_spec[1] if conjugate else first_spec[1]
    return jnp.stack(
        [
            first_spec[0] * second_spec[0] - imag_first * second_spec[1],
            first_spec[0] * second_spec[1] + imag_first * second_spec[0],
        ]
    )


def block_angles(block_size, inner_size, seq_rows, direction):
    outer_iota = lax.broadcasted_iota(jnp.int32, (block_size, inner_size), 0)
    inner_iota = lax.broadcasted_iota(jnp.int32, (block_size, inner_size), 1)
    rotation = (
        direction
        * 2.0
        * math.pi
        / seq_rows
        * (outer_iota * inner_iota % seq_rows).astype(jnp.float32)
    )
    return (jnp.cos(rotation)[:, :, None], jnp.sin(rotation)[:, :, None])


def local_forward(columns, block_size):
    seq_rows = columns.shape[1]
    item_width = columns.shape[2]
    inner_size = seq_rows // block_size
    shaped = columns.reshape(2, block_size, inner_size, item_width)
    first_pass = jnp.einsum(
        "xabz,xayk->ykbz",
        shaped,
        complex_table(block_size, block_size, block_size, -1.0),
        precision=HIGHEST,
    )
    cosine, sine_part = block_angles(block_size, inner_size, seq_rows, -1.0)
    rotated = rotate(first_pass, cosine, sine_part)
    second = jnp.einsum(
        "ykbz,ybwm->wkmz",
        rotated,
        complex_table(inner_size, inner_size, inner_size, -1.0),
        precision=HIGHEST,
    )
    return second.reshape(2, seq_rows, item_width)


def local_inverse(columns, block_size):
    seq_rows = columns.shape[1]
    item_width = columns.shape[2]
    inner_size = seq_rows // block_size
    shaped = columns.reshape(2, block_size, inner_size, item_width)
    first_pass = jnp.einsum(
        "xkmz,xmyb->ykbz",
        shaped,
        complex_table(inner_size, inner_size, inner_size, 1.0),
        precision=HIGHEST,
    )
    cosine, sine_part = block_angles(block_size, inner_size, seq_rows, 1.0)
    rotated = rotate(first_pass, cosine, sine_part)
    second = jnp.einsum(
        "xkbz,xkya->yabz",
        rotated,
        complex_table(block_size, block_size, block_size, 1.0),
        precision=HIGHEST,
    )
    return second.reshape(2, seq_rows, item_width) * (1.0 / seq_rows)


def cross_transform(columns, dft_table):
    seq_rows = columns.shape[1]
    item_width = columns.shape[2]
    shaped = columns.reshape(2, 1, seq_rows, item_width)
    transformed = jnp.einsum(
        "xpjz,xpyk->ykjz",
        lax.all_to_all(shaped, "seq", split_axis=2, concat_axis=1, tiled=True),
        dft_table,
        precision=HIGHEST,
    )
    result = lax.all_to_all(transformed, "seq", split_axis=1, concat_axis=2, tiled=True)
    return result.reshape(2, seq_rows, item_width)


def shard_twiddle(columns, frequency, seq_length, direction):
    seq_rows = columns.shape[1]
    local_pos = jnp.arange(seq_rows, dtype=jnp.int32)
    rotation = (
        direction
        * 2.0
        * math.pi
        / seq_length
        * (local_pos * frequency % seq_length).astype(jnp.float32)
    )
    return rotate(columns, jnp.cos(rotation)[:, None], jnp.sin(rotation)[:, None])


def forward(columns, shard_index, devices, block_size):
    seq_length = columns.shape[1] * devices
    columns = cross_transform(columns, complex_table(devices, devices, devices, -1.0))
    columns = shard_twiddle(columns, shard_index, seq_length, -1.0)
    return local_forward(columns, block_size)


def inverse(columns, shard_index, devices, block_size):
    seq_length = columns.shape[1] * devices
    columns = local_inverse(columns, block_size)
    columns = shard_twiddle(columns, shard_index, seq_length, 1.0)
    columns = cross_transform(
        columns, complex_table(devices, devices, devices, 1.0) * (1.0 / devices)
    )
    return columns


def per_device(inputs, value_weight, query_weight, filters, grad_out):
    channel_count = filters.shape[0]
    seq_rows = filters.shape[1]
    devices = lax.axis_size("seq")
    shard_index = lax.axis_index("seq")
    seq_length = seq_rows * devices
    grad_scale = 1.0 / math.sqrt(seq_length)
    all_inputs = lax.all_gather(inputs, "chan", axis=0, tiled=True)
    projected = jnp.einsum("cd,ct->dt", value_weight, all_inputs, precision=HIGHEST)
    query_proj = jnp.einsum("cd,ct->dt", query_weight, all_inputs, precision=HIGHEST)
    gated_grad = grad_out * query_proj
    signals = jnp.stack([projected, filters, gated_grad])
    position = shard_index * seq_rows + jnp.arange(seq_rows, dtype=jnp.int32)
    twist_angle = 0.5 * math.pi / seq_length * position.astype(jnp.float32)
    cosine = jnp.cos(twist_angle)
    sine_part = jnp.sin(twist_angle)
    twisted = jnp.stack([signals * cosine, -signals * sine_part])
    columns = jnp.transpose(twisted, (0, 3, 1, 2)).reshape(2, seq_rows, 3 * channel_count)
    spectra = forward(columns, shard_index, devices, BLK).reshape(2, seq_rows, 3, channel_count)
    value_spec = spectra[:, :, 0]
    filter_spec = spectra[:, :, 1]
    grad_spec = spectra[:, :, 2]
    products = jnp.stack(
        [
            multiply(filter_spec, value_spec, False),
            multiply(filter_spec, grad_spec, True),
            multiply(value_spec, grad_spec, True),
        ],
        axis=2,
    )
    restored = inverse(
        products.reshape(2, seq_rows, 3 * channel_count), shard_index, devices, BLK
    ).reshape(2, seq_rows, 3, channel_count)
    combined = restored[0] * cosine[:, None, None] - restored[1] * sine_part[:, None, None]
    combined = jnp.transpose(combined, (1, 2, 0))
    convolved = combined[0]
    grad_value = combined[1]
    filter_grad = combined[2] * grad_scale
    grad_query = grad_out * convolved
    input_grad = lax.psum_scatter(
        jnp.dot(value_weight, grad_value, precision=HIGHEST, preferred_element_type=jnp.float32)
        + jnp.dot(query_weight, grad_query, precision=HIGHEST, preferred_element_type=jnp.float32),
        "chan",
        scatter_dimension=0,
        tiled=True,
    )
    partial_value = jnp.einsum("ct,dt->cd", all_inputs, grad_value, precision=HIGHEST) * grad_scale
    partial_query = jnp.einsum("ct,dt->cd", all_inputs, grad_query, precision=HIGHEST) * grad_scale
    value_gradient, query_gradient = lax.psum((partial_value, partial_query), "seq")
    return (input_grad, filter_grad, value_gradient, query_gradient)


NN = (((1,), (0,)), ((), ()))
NT = (((1,), (1,)), ((), ()))


def split_table(table):
    high = table.astype(jnp.bfloat16)
    low = (table - high.astype(np.float32)).astype(jnp.bfloat16)
    return high, low


@functools.lru_cache(maxsize=None)
def transform_tables(seq_length):
    outer = seq_length // LANES
    k = np.arange(outer, dtype=np.float64)
    a = np.arange(outer, dtype=np.float64)
    b = np.arange(LANES, dtype=np.float64)
    phase = 2 * np.pi * np.outer(4 * k + 1, a) % (2 * np.pi * 4 * outer) / (4 * outer)
    small = np.concatenate([np.cos(phase), -np.sin(phase)], axis=0)
    wide = np.repeat(small, GROUP, axis=0).astype(np.float32)
    tall = (np.repeat(small.T, GROUP, axis=0) / seq_length).astype(np.float32)
    angle = 2 * np.pi * np.repeat(np.outer(4 * k + 1, b), GROUP, axis=0) / (4 * seq_length)
    turn = np.stack([np.cos(angle), np.sin(angle)]).astype(np.float32)
    inner = 2 * np.pi * (np.outer(b, b) % LANES) / LANES
    c, s = np.cos(inner), np.sin(inner)
    ahead = np.block([[c, -s], [s, c]]).astype(np.float32)
    back = np.block([[c, s], [-s, c]]).astype(np.float32)
    return (
        *split_table(wide),
        *split_table(tall),
        *split_table(ahead),
        *split_table(back),
        turn,
    )


def split(x):
    high = x.astype(jnp.bfloat16)
    return high, (x - high.astype(jnp.float32)).astype(jnp.bfloat16)


def dot3(first, second, dims=NN):
    def dot(x, y):
        return lax.dot_general(x, y, dims, preferred_element_type=jnp.float32)

    return dot(first[0], second[0]) + (dot(first[0], second[1]) + dot(first[1], second[0]))


def spread(small_ref, out_ref):
    rows, cols = out_ref.shape
    inner = small_ref.shape[1]
    pick = lax.broadcasted_iota(jnp.int32, (inner, cols), 1) // GROUP
    own = lax.broadcasted_iota(jnp.int32, (inner, cols), 0)
    picks = jnp.where(pick == own, 1.0, 0.0).astype(jnp.bfloat16)
    row_lane = lax.broadcasted_iota(jnp.int32, (rows, cols), 0) % GROUP
    col_lane = lax.broadcasted_iota(jnp.int32, (rows, cols), 1) % GROUP
    full = lax.dot_general(small_ref[...], picks, NN, preferred_element_type=jnp.float32)
    out_ref[...] = jnp.where(row_lane == col_lane, full, 0.0).astype(jnp.bfloat16)


def fused_kernel(devices, scale, *refs):
    x_hbm, vw_hbm, qw_hbm, f_hbm, g_hbm = refs[:5]
    table_hbm = refs[5:14]
    ig_out, fg_out, vg_out, qg_out = refs[14:18]
    x_ref, vw_ref, qw_ref, g_ref = refs[18:22]
    small_refs = refs[22:26]
    ahead_h, ahead_l, back_h, back_l, turn_ref = refs[26:31]
    wide_h, wide_l, tall_h, tall_l = refs[31:35]
    other_x, send_sig, in_sig, spec, out_sig, ret_sig, part, scat, red, gath = refs[35:45]
    ig_send, ig_recv, ssem, rsem, csend, crecv, lsem = refs[45:]
    me = lax.axis_index("seq")
    chan = lax.axis_index("chan")
    half, width = x_ref.shape
    pieces = width // LANES
    inner = 1 << (devices.bit_length() - 1) // 2
    outer = devices // inner
    rows = 2 * half // inner
    me_inner, me_outer = me % inner, me // inner

    def peer_of(i):
        peer, bit = me, 1
        while bit < devices:
            peer = peer + (i // bit) % 2 * (1 - 2 * (me // bit % 2)) * bit
            bit *= 2
        return peer

    barrier = pltpu.get_barrier_semaphore()

    def greet(i, carry):
        pl.semaphore_signal(
            barrier,
            inc=1,
            device_id={"seq": peer_of(devices - i)},
            device_id_type=pl.DeviceIdType.MESH,
        )
        return carry

    lax.fori_loop(1, devices, greet, 0)
    pl.semaphore_signal(
        barrier, inc=1, device_id={"chan": 1 - chan}, device_id_type=pl.DeviceIdType.MESH
    )

    loads = [
        pltpu.make_async_copy(src, dst, lsem.at[at])
        for at, (src, dst) in enumerate(
            zip(
                (x_hbm, vw_hbm, qw_hbm, g_hbm, *table_hbm),
                (x_ref, vw_ref, qw_ref, g_ref, *small_refs)
                + (ahead_h, ahead_l, back_h, back_l, turn_ref),
            )
        )
    ]
    for load in loads:
        load.start()
    own_f = pl.ds(pl.multiple_of(me * GROUP, GROUP), GROUP)
    keep_f = pltpu.make_async_copy(f_hbm.at[own_f, :], in_sig.at[0, me], lsem.at[len(loads)])
    keep_f.start()
    for load in loads[:3]:
        load.wait()

    own_rows = pl.ds(pl.multiple_of(chan * half, half), half)
    other_rows = pl.ds(pl.multiple_of((1 - chan) * half, half), half)
    own_x = split(x_ref[...])
    partial_value = dot3(split(vw_ref[own_rows, :].T), own_x)
    partial_query = dot3(split(qw_ref[own_rows, :].T), own_x)

    pl.semaphore_wait(barrier, devices)

    def exchange(index, src, dst):
        return pltpu.make_async_remote_copy(
            src_ref=src,
            dst_ref=dst,
            send_sem=csend.at[index],
            recv_sem=crecv.at[index],
            device_id={"chan": 1 - chan},
            device_id_type=pl.DeviceIdType.MESH,
        )

    def each(slot, src_of, dst_of, what, count=devices, stride=1):
        def step(i, carry):
            index = (count - i) * stride
            peer = peer_of(index)
            copy = pltpu.make_async_remote_copy(
                src_ref=src_of(peer),
                dst_ref=dst_of(),
                send_sem=ssem.at[slot, index],
                recv_sem=rsem.at[slot, index],
                device_id={"seq": peer},
                device_id_type=pl.DeviceIdType.MESH,
            )
            getattr(copy, what)()
            return carry

        lax.fori_loop(1, count, step, 0)

    def group_rows(peer, count):
        return pl.ds(pl.multiple_of(peer * count, count), count)

    def out_way(slot, what):
        src = f_hbm if slot == 0 else send_sig.at[slot - 1]
        each(slot, lambda p: src.at[group_rows(p, GROUP), :], lambda: in_sig.at[slot, me], what)

    def back_way(slot, what):
        each(
            3 + slot,
            lambda p: out_sig.at[slot, p],
            lambda: ret_sig.at[slot, group_rows(me, GROUP), :],
            what,
        )

    def scatter(slot, what):
        each(
            6 + slot,
            lambda p: part.at[slot, group_rows(p % inner, rows), :],
            lambda: scat.at[slot, me_inner],
            what,
            inner,
        )

    def swap(slot, what):
        each(
            8 + slot,
            lambda p: red.at[slot, me_outer],
            lambda: red.at[slot, me_outer],
            what,
            outer,
            inner,
        )

    def gather(slot, what):
        each(
            10 + slot,
            lambda p: gath.at[slot, group_rows(me_inner, rows), :],
            lambda: gath.at[slot, group_rows(me_inner, rows), :],
            what,
            inner,
        )

    give_x = exchange(0, x_hbm, other_x)
    give_x.start()
    out_way(0, "start")
    give_x.wait()

    far_x = split(other_x[...])
    send_sig[0] = partial_value + dot3(split(vw_ref[other_rows, :].T), far_x)
    out_way(1, "start")
    in_sig[1, me] = send_sig[0, group_rows(me, GROUP), :]
    query_proj = partial_query + dot3(split(qw_ref[other_rows, :].T), far_x)
    loads[3].wait()
    send_sig[1] = g_ref[...] * query_proj
    out_way(2, "start")
    in_sig[2, me] = send_sig[1, group_rows(me, GROUP), :]

    for load in loads[4:]:
        load.wait()
    for small_ref, out_ref in zip(small_refs, (wide_h, wide_l, tall_h, tall_l)):
        spread(small_ref, out_ref)
    keep_f.wait()
    wide = (wide_h[...], wide_l[...])
    tall = (tall_h[...], tall_l[...])
    ahead = (ahead_h[...], ahead_l[...])
    back = (back_h[...], back_l[...])
    cosine = turn_ref[0]
    sine = turn_ref[1]
    count = cosine.shape[0]

    def transform(slot):
        signal = jnp.concatenate(
            [
                in_sig[slot, source, :, piece * LANES : (piece + 1) * LANES]
                for source in range(devices)
                for piece in range(pieces)
            ],
            axis=0,
        )
        first = dot3(wide, split(signal))
        real, imag = first[:count], first[count:]
        turned = jnp.concatenate(
            [real * cosine + imag * sine, imag * cosine - real * sine], axis=1
        )
        spec[slot] = dot3(split(turned), ahead)

    def restore(first, second, conjugate, slot):
        real_a, imag_a = spec[first, :, :LANES], spec[first, :, LANES:]
        real_b, imag_b = spec[second, :, :LANES], spec[second, :, LANES:]
        if conjugate:
            imag_a = -imag_a
        product = jnp.concatenate(
            [real_a * real_b - imag_a * imag_b, real_a * imag_b + imag_a * real_b], axis=1
        )
        inner = dot3(split(product), back)
        real, imag = inner[:, :LANES], inner[:, LANES:]
        turned = jnp.concatenate(
            [real * cosine - imag * sine, imag * cosine + real * sine], axis=0
        )
        signal = dot3(tall, split(turned))
        if slot == 2:
            signal = signal * scale
        for target in range(devices):
            for piece in range(pieces):
                at = (target * pieces + piece) * GROUP
                out_sig[slot, target, :, piece * LANES : (piece + 1) * LANES] = signal[
                    at : at + GROUP
                ]
        back_way(slot, "start")
        ret_sig[slot, group_rows(me, GROUP), :] = out_sig[slot, me]

    out_way(0, "wait_recv")
    transform(0)
    out_way(1, "wait_recv")
    transform(1)
    restore(0, 1, False, 0)
    out_way(2, "wait_recv")
    transform(2)
    restore(0, 2, True, 1)
    restore(1, 2, True, 2)

    def weight_part(slot, grad):
        part[slot, own_rows, :] = dot3(own_x2, grad, NT)
        part[slot, other_rows, :] = dot3(far_x2, grad, NT)
        scatter(slot, "start")
        scat[slot, me_inner] = part[slot, group_rows(me_inner, rows), :]

    own_x2 = split(x_ref[...])
    far_x2 = split(other_x[...])
    back_way(0, "wait_recv")
    grad_query = split(g_ref[...] * ret_sig[0])
    weight_part(0, grad_query)
    near_grad = dot3(split(qw_ref[own_rows, :]), grad_query)
    far_grad = dot3(split(qw_ref[other_rows, :]), grad_query)

    def reduce_inner(slot):
        scatter(slot, "wait_recv")
        total = scat[slot, 0]
        for source in range(1, inner):
            total = total + scat[slot, source]
        red[slot, me_outer] = total
        swap(slot, "start")

    def reduce_outer(slot):
        swap(slot, "wait_recv")
        total = red[slot, 0]
        for source in range(1, outer):
            total = total + red[slot, source]
        gath[slot, group_rows(me_inner, rows), :] = total * scale
        gather(slot, "start")

    reduce_inner(0)
    back_way(1, "wait_recv")
    grad_value = split(ret_sig[1])
    weight_part(1, grad_value)
    ig_send[...] = far_grad + dot3(split(vw_ref[other_rows, :]), grad_value)
    give_ig = exchange(1, ig_send, ig_recv)
    give_ig.start()
    reduce_inner(1)
    near_grad = near_grad + dot3(split(vw_ref[own_rows, :]), grad_value)
    reduce_outer(0)
    give_ig.wait()
    ig_out[...] = near_grad + ig_recv[...]
    reduce_outer(1)
    back_way(2, "wait_recv")
    fg_out[...] = ret_sig[2]
    for slot, out in ((0, qg_out), (1, vg_out)):
        gather(slot, "wait_recv")
        out[...] = gath[slot]
    for slot in range(3):
        out_way(slot, "wait_send")
        back_way(slot, "wait_send")
    for slot in range(2):
        scatter(slot, "wait_send")
        swap(slot, "wait_send")
        gather(slot, "wait_send")


def finish_kernel(*refs):
    stores = [
        pltpu.make_async_copy(source, target, refs[8].at[at])
        for at, (source, target) in enumerate(zip(refs[:4], refs[4:8]))
    ]
    for store in stores:
        store.start()
    for store in stores:
        store.wait()


def fused_device(inputs, value_weight, query_weight, filters, grad_out):
    half, width = inputs.shape
    devices = lax.axis_size("seq")
    seq_length = width * devices
    depth = value_weight.shape[0]
    inner = 1 << (devices.bit_length() - 1) // 2
    outer = devices // inner
    rows = depth // inner
    tables = transform_tables(seq_length)
    count = seq_length // LANES * GROUP
    tables = [jnp.asarray(t) for t in tables]
    hbm = pl.BlockSpec(memory_space=pltpu.HBM)
    vmem = pl.BlockSpec(memory_space=pltpu.VMEM)
    f32, bf16 = jnp.float32, jnp.bfloat16
    outs = (
        jax.ShapeDtypeStruct((half, width), f32),
        jax.ShapeDtypeStruct((half, width), f32),
        jax.ShapeDtypeStruct((depth, half), f32),
        jax.ShapeDtypeStruct((depth, half), f32),
    )
    results = pl.pallas_call(
        functools.partial(fused_kernel, devices, 1.0 / math.sqrt(seq_length)),
        out_shape=tuple(pltpu.VMEM(out.shape, out.dtype) for out in outs),
        in_specs=[hbm] * (5 + len(tables)),
        out_specs=(vmem,) * 4,
        scratch_shapes=[
            pltpu.VMEM((half, width), f32),
            pltpu.VMEM((depth, half), f32),
            pltpu.VMEM((depth, half), f32),
            pltpu.VMEM((half, width), f32),
            *(pltpu.VMEM(t.shape, t.dtype) for t in tables),
            pltpu.VMEM((2 * count, count), bf16),
            pltpu.VMEM((2 * count, count), bf16),
            pltpu.VMEM((count, 2 * count), bf16),
            pltpu.VMEM((count, 2 * count), bf16),
            pltpu.VMEM((half, width), f32),
            pltpu.VMEM((2, half, width), f32),
            pltpu.VMEM((3, devices, GROUP, width), f32),
            pltpu.VMEM((3, count, 2 * LANES), f32),
            pltpu.VMEM((3, devices, GROUP, width), f32),
            pltpu.VMEM((3, half, width), f32),
            pltpu.VMEM((2, depth, half), f32),
            pltpu.VMEM((2, inner, rows, half), f32),
            pltpu.VMEM((2, outer, rows, half), f32),
            pltpu.VMEM((2, depth, half), f32),
            pltpu.VMEM((half, width), f32),
            pltpu.VMEM((half, width), f32),
            pltpu.SemaphoreType.DMA((12, devices)),
            pltpu.SemaphoreType.DMA((12, devices)),
            pltpu.SemaphoreType.DMA((2,)),
            pltpu.SemaphoreType.DMA((2,)),
            pltpu.SemaphoreType.DMA((5 + len(tables),)),
        ],
        compiler_params=pltpu.CompilerParams(
            collective_id=0, has_side_effects=True, vmem_limit_bytes=60 * 1024 * 1024
        ),
    )(inputs, value_weight, query_weight, filters, grad_out, *tables)
    return tuple(
        pl.pallas_call(
            finish_kernel,
            out_shape=outs,
            in_specs=[vmem] * 4,
            out_specs=(hbm,) * 4,
            scratch_shapes=[pltpu.SemaphoreType.DMA((4,))],
        )(*(pltpu.with_memory_space_constraint(r, pltpu.VMEM) for r in results))
    )


def on_device(inputs, value_weight, query_weight, filters, grad_out):
    channel_count, width = filters.shape
    devices = lax.axis_size("seq")
    fits = (
        channel_count == GROUP * devices
        and channel_count == inputs.shape[0]
        and lax.axis_size("chan") == 2
        and width % LANES == 0
        and channel_count % LANES == 0
        and devices & (devices - 1) == 0
        and value_weight.shape[0] % (GROUP * devices) == 0
    )
    body = fused_device if fits else per_device
    return body(inputs, value_weight, query_weight, filters, grad_out)


def solution(mesh):
    return jax.shard_map(
        on_device,
        mesh=mesh,
        in_specs=(
            P("chan", "seq"),
            P(None, "chan"),
            P(None, "chan"),
            P("chan", "seq"),
            P("chan", "seq"),
        ),
        out_specs=(P("chan", "seq"), P("chan", "seq"), P(None, "chan"), P(None, "chan")),
        check_vma=False,
    )
```
